32 devices in a mesh: league: 4 (over x, core), env: 8 (over z, y).
Axes of the slice: x: 2, y: 2, z: 4, core: 2. Of those that a mesh axis runs over, the one named last changes fastest.
Arguments:
- obs_own: bfloat16 [4, 2, 128, 16, 2048], P('league', None, 'env'), may hold values from -6 to 6
- obs_opp: bfloat16 [4, 2, 128, 16, 2048], P('league', None, 'env'), may hold values from -6 to 6
- actions: int32 [4, 2, 2, 128, 16], P('league', None, None, 'env'), may hold values from 0 to 255
- opponent_picks: int32 [4, 2], P('league'), may hold values from 0 to 3
- policy_weight: bfloat16 [4, 2048, 2048], P('league', 'env'), may hold values from -0.125 to 0.125
- policy_gain: bfloat16 [4, 2048], P('league'), may hold values from 0.25 to 1.75
- action_table: bfloat16 [256, 2048], replicated, may hold values from -6 to 6
- value_gain: bfloat16 [2048], replicated, may hold values from 0.25 to 1.75
- value_up: bfloat16 [2048, 1024], replicated, may hold values from -0.125 to 0.125
- value_out: bfloat16 [1024], replicated, may hold values from -0.1875 to 0.1875
Outputs:
- learner_rows: bfloat16 [4, 2, 16, 2048, 128], P('league', None, None, 'env')
- values: float32 [4, 2, 128, 16], P('league', None, 'env')
The draws below stay inside these ranges and needn't reach their ends.
All inputs are finite; a program needn't handle non-finite values.
Results may differ from the reference program's by a relative error of at most 0.0054.
Values may be sent and summed in bfloat16 or wider, within the bound.
A program may use at most 128 MiB of HBM per device.

```python
import jax
import jax.numpy as jnp
from jax import lax

D = 2048
VH = 1024
ACTIONS = 256
STEPS = 16
ROUNDS = 2
GROUPS = 4
ENVS = 128


def with_ends(array, rng, low, high):
    place = [jax.random.randint(jax.random.fold_in(rng, axis), (), 0, length) for axis, length in enumerate(array.shape)]
    widest = array.shape.index(max(array.shape))
    beside = place[:widest] + [(place[widest] + 1) % array.shape[widest]] + place[widest + 1:]
    return array.at[tuple(place)].set(low).at[tuple(beside)].set(high)


def steps_of(key, extent, shards, low, top_value):
    def one(dim, blocks):
        steps = jax.random.uniform(jax.random.fold_in(jax.random.fold_in(key, 6), dim), (blocks,), jnp.float32, low / len(shards), top_value / len(shards))
        return jnp.repeat(jnp.exp(steps), extent[dim] // blocks).reshape((-1,) + (1,) * (len(extent) - dim - 1))

    loudness = one(*shards[0])
    for cut in shards[1:]:
        loudness = loudness * one(*cut)
    return loudness


def centred(own_key, extent, width, most, pieces=(), held_as=jnp.bfloat16):
    values = jax.random.normal(own_key, extent, jnp.float32) * width
    if len(pieces) > 0:
        values = steps_of(own_key, extent, pieces, -0.22, 0.18) * values
    return jnp.clip(values, min=-most, max=most).astype(held_as)


def setup_inputs(seed: int = 0) -> dict:
    arg_keys = jax.random.split(jax.random.key(seed), 11)
    obs_own = centred(arg_keys[0], (GROUPS, ROUNDS, ENVS, STEPS, D), 1.0, 6.0, ((0, 4), (2, 8)))
    obs_opp = centred(arg_keys[1], (GROUPS, ROUNDS, ENVS, STEPS, D), 1.0, 6.0, ((0, 4), (2, 8)))
    actions = with_ends(jax.random.randint(arg_keys[2], (GROUPS, 2, ROUNDS, ENVS, STEPS), 0, ACTIONS), jax.random.fold_in(arg_keys[2], 1), 0, ACTIONS - 1).astype(jnp.int32)
    opponent_picks = with_ends(jax.random.randint(arg_keys[3], (GROUPS, ROUNDS), 0, GROUPS), jax.random.fold_in(arg_keys[3], 1), 0, GROUPS - 1).astype(jnp.int32)
    policy_weight = centred(arg_keys[4], (GROUPS, D, D), D ** -0.5, 0.125, ((0, 4), (1, 8)))
    policy_gain = jnp.clip(1.0 + 0.15 * jax.random.normal(arg_keys[5], (GROUPS, D), jnp.float32), 0.25, 1.75).astype(jnp.bfloat16)
    action_table = centred(arg_keys[6], (ACTIONS, D), 1.0, 6.0)
    value_gain = jnp.clip(1.0 + 0.15 * jax.random.normal(arg_keys[7], (D,), jnp.float32), 0.25, 1.75).astype(jnp.bfloat16)
    value_up = centred(arg_keys[8], (D, VH), D ** -0.5, 0.125)
    value_out = centred(arg_keys[9], (VH,), VH ** -0.5, 0.1875)
    return {"obs_own": obs_own, "obs_opp": obs_opp, "actions": actions, "opponent_picks": opponent_picks, "policy_weight": policy_weight, "policy_gain": policy_gain, "action_table": action_table, "value_gain": value_gain, "value_up": value_up, "value_out": value_out}


def rms_norm(inputs, gain):
    scale = lax.rsqrt(lax.optimization_barrier(jnp.mean(inputs * inputs, axis=-1, keepdims=True)) + 1e-05)
    return inputs * scale * gain.astype(jnp.float32)

def policy(inputs, weight, gain):
    values_f = inputs.astype(jnp.float32)
    normed = rms_norm(values_f, gain).astype(jnp.bfloat16)
    return values_f + jnp.dot(normed, weight, preferred_element_type=jnp.float32)

def reference(obs_own, obs_opp, actions, opponent_picks, policy_weight, policy_gain, action_table, value_gain, value_up, value_out):
    row_count = ENVS * STEPS

    def one_group(group_index):
        traj_list = []
        value_list = []
        for round_index in range(ROUNDS):
            opp_index = opponent_picks[group_index, round_index]
            own_state = policy(obs_own[group_index, round_index].reshape(row_count, D), policy_weight[group_index], policy_gain[group_index])
            opp_state = policy(obs_opp[group_index, round_index].reshape(row_count, D), policy_weight[opp_index], policy_gain[opp_index])
            own_ids = actions[group_index, 0, round_index].reshape(row_count)
            opp_ids = actions[group_index, 1, round_index].reshape(row_count)
            action_sum = action_table[own_ids].astype(jnp.float32) + action_table[opp_ids].astype(jnp.float32)
            joint_sum = own_state + opp_state + action_sum
            joint_row = rms_norm(joint_sum, value_gain).astype(jnp.bfloat16)
            value_hidden = jax.nn.silu(jnp.dot(joint_row, value_up, preferred_element_type=jnp.float32)).astype(jnp.bfloat16)
            value_est = jnp.dot(value_hidden, value_out, preferred_element_type=jnp.float32)
            value_list.append(value_est.reshape(ENVS, STEPS))
            traj_list.append(joint_row.reshape(ENVS, STEPS, D).transpose(1, 2, 0))
        return (jnp.stack(traj_list), jnp.stack(value_list))
    learner_rows, values = lax.map(one_group, jnp.arange(GROUPS, dtype=jnp.int32))
    return (learner_rows, values)
```

```python
import jax
import jax.numpy as jnp
from jax import lax
from jax.sharding import PartitionSpec as P


def rms_norm(inputs, gain):
    scale = lax.rsqrt(jnp.mean(inputs * inputs, axis=-1, keepdims=True) + 1e-05)
    return inputs * scale * gain.astype(jnp.float32)


def local(
    obs_own,
    obs_opp,
    actions,
    opponent_picks,
    policy_weight,
    policy_gain,
    action_table,
    value_gain,
    value_up,
    value_out,
):
    round_count = obs_own.shape[1]
    env_count = obs_own.shape[2]
    step_count = obs_own.shape[3]
    model_width = obs_own.shape[4]
    row_count = env_count * step_count
    weight_shard = policy_weight[0]
    own_gain = policy_gain[0]
    group_count = lax.axis_size("league")
    my_group = lax.axis_index("league")
    own_inputs = obs_own[0].reshape(round_count * row_count, model_width).astype(jnp.float32)
    own_normed = rms_norm(own_inputs, own_gain).astype(jnp.bfloat16)
    own_whole = lax.all_gather(weight_shard, "env", axis=0, tiled=True)
    own_state = own_inputs + jnp.dot(own_normed, own_whole, preferred_element_type=jnp.float32)
    every_pick = lax.all_gather(opponent_picks, "league", axis=0, tiled=True)
    action_range = jnp.arange(action_table.shape[0], dtype=jnp.int32)
    traj_list = []
    value_list = []
    for round_index in range(round_count):
        opp_raw = obs_opp[0, round_index].reshape(row_count, model_width)
        opp_inputs = opp_raw.astype(jnp.float32)
        all_rows = lax.all_gather(opp_raw, "league", axis=0, tiled=True)
        all_normed = rms_norm(all_rows.astype(jnp.float32), own_gain).astype(jnp.bfloat16)
        products = jnp.dot(all_normed, own_whole, preferred_element_type=jnp.float32)
        served = (every_pick[:, round_index] == my_group).astype(jnp.float32)
        products = (
            products.reshape(group_count, row_count, model_width) * served[:, None, None]
        ).astype(jnp.bfloat16)
        answers = lax.all_to_all(products, "league", split_axis=0, concat_axis=0, tiled=True)
        opp_state = opp_inputs + jnp.sum(answers.astype(jnp.float32), axis=0)
        own_ids = actions[0, 0, round_index].reshape(row_count)
        opp_ids = actions[0, 1, round_index].reshape(row_count)
        onehot = (own_ids[:, None] == action_range[None, :]).astype(jnp.bfloat16) + (
            opp_ids[:, None] == action_range[None, :]
        ).astype(jnp.bfloat16)
        action_sum = jnp.dot(onehot, action_table, preferred_element_type=jnp.float32)
        round_state = lax.dynamic_slice_in_dim(own_state, round_index * row_count, row_count, 0)
        joint_sum = round_state + opp_state + action_sum
        joint_row = rms_norm(joint_sum, value_gain).astype(jnp.bfloat16)
        value_hidden = jax.nn.silu(
            jnp.dot(joint_row, value_up, preferred_element_type=jnp.float32)
        ).astype(jnp.bfloat16)
        value_est = jnp.dot(value_hidden, value_out, preferred_element_type=jnp.float32)
        value_list.append(value_est.reshape(env_count, step_count))
        time_block = joint_row.reshape(env_count, step_count, model_width).transpose(1, 2, 0)
        traj_list.append(lax.all_to_all(time_block, "env", split_axis=1, concat_axis=2, tiled=True))
    learner_rows = jnp.stack(traj_list)
    values = jnp.stack(value_list)
    return (learner_rows[None], values[None])


def solution(mesh):
    in_specs = (
        P("league", None, "env", None, None),
        P("league", None, "env", None, None),
        P("league", None, None, "env", None),
        P("league", None),
        P("league", "env", None),
        P("league", None),
        P(),
        P(),
        P(),
        P(),
    )
    out_specs = (P("league", None, None, "env", None), P("league", None, "env", None))
    return jax.shard_map(local, mesh=mesh, in_specs=in_specs, out_specs=out_specs, check_vma=False)
```

```python
import functools

import jax
import jax.numpy as jnp
from jax import lax
from jax.experimental import pallas as pl
from jax.experimental.pallas import tpu as pltpu
from jax.sharding import PartitionSpec as P

F32 = jnp.float32
BF16 = jnp.bfloat16
BLOCKS = 4
LINE = 4
PAIR = 2
MIB = 1 << 20


def rms_norm(inputs, gain):
    scale = lax.rsqrt(jnp.mean(inputs * inputs, axis=-1, keepdims=True) + 1e-05)
    return inputs * scale * gain.astype(jnp.float32)


def local(
    obs_own,
    obs_opp,
    actions,
    opponent_picks,
    policy_weight,
    policy_gain,
    action_table,
    value_gain,
    value_up,
    value_out,
):
    round_count = obs_own.shape[1]
    env_count = obs_own.shape[2]
    step_count = obs_own.shape[3]
    model_width = obs_own.shape[4]
    row_count = env_count * step_count
    weight_shard = policy_weight[0]
    own_gain = policy_gain[0]
    group_count = lax.axis_size("league")
    my_group = lax.axis_index("league")
    own_inputs = obs_own[0].reshape(round_count * row_count, model_width).astype(jnp.float32)
    own_normed = rms_norm(own_inputs, own_gain).astype(jnp.bfloat16)
    own_whole = lax.all_gather(weight_shard, "env", axis=0, tiled=True)
    own_state = own_inputs + jnp.dot(own_normed, own_whole, preferred_element_type=jnp.float32)
    every_pick = lax.all_gather(opponent_picks, "league", axis=0, tiled=True)
    action_range = jnp.arange(action_table.shape[0], dtype=jnp.int32)
    traj_list = []
    value_list = []
    for round_index in range(round_count):
        opp_raw = obs_opp[0, round_index].reshape(row_count, model_width)
        opp_inputs = opp_raw.astype(jnp.float32)
        all_rows = lax.all_gather(opp_raw, "league", axis=0, tiled=True)
        all_normed = rms_norm(all_rows.astype(jnp.float32), own_gain).astype(jnp.bfloat16)
        products = jnp.dot(all_normed, own_whole, preferred_element_type=jnp.float32)
        served = (every_pick[:, round_index] == my_group).astype(jnp.float32)
        products = (
            products.reshape(group_count, row_count, model_width) * served[:, None, None]
        ).astype(jnp.bfloat16)
        answers = lax.all_to_all(products, "league", split_axis=0, concat_axis=0, tiled=True)
        opp_state = opp_inputs + jnp.sum(answers.astype(jnp.float32), axis=0)
        own_ids = actions[0, 0, round_index].reshape(row_count)
        opp_ids = actions[0, 1, round_index].reshape(row_count)
        onehot = (own_ids[:, None] == action_range[None, :]).astype(jnp.bfloat16) + (
            opp_ids[:, None] == action_range[None, :]
        ).astype(jnp.bfloat16)
        action_sum = jnp.dot(onehot, action_table, preferred_element_type=jnp.float32)
        round_state = lax.dynamic_slice_in_dim(own_state, round_index * row_count, row_count, 0)
        joint_sum = round_state + opp_state + action_sum
        joint_row = rms_norm(joint_sum, value_gain).astype(jnp.bfloat16)
        value_hidden = jax.nn.silu(
            jnp.dot(joint_row, value_up, preferred_element_type=jnp.float32)
        ).astype(jnp.bfloat16)
        value_est = jnp.dot(value_hidden, value_out, preferred_element_type=jnp.float32)
        value_list.append(value_est.reshape(env_count, step_count))
        time_block = joint_row.reshape(env_count, step_count, model_width).transpose(1, 2, 0)
        traj_list.append(lax.all_to_all(time_block, "env", split_axis=1, concat_axis=2, tiled=True))
    learner_rows = jnp.stack(traj_list)
    values = jnp.stack(value_list)
    return (learner_rows[None], values[None])


def window_kernel(
    w_ref, own_ref, opp_ref, onehot_ref, picks_ref, gain_ref, table_ref, vgain_ref, up_ref, vout_ref,
    out_ref, val_ref,
    wbuf, rows, own_n, joint, to_sib, from_sib, to_x, from_x, picks_all, jrow, jsend, arecv,
    w_send, w_recv, o_send, o_recv, p_send, p_recv, s_send, s_recv, x_send, x_recv, a_send, a_recv,
):
    blocks, env, depth, width = wbuf.shape
    rounds, count, model = own_ref.shape
    steps, envs = arecv.shape[1], arecv.shape[3]
    league_me = lax.axis_index("league")
    me = lax.axis_index("env")
    x, core = league_me // 2, league_me % 2
    z, y = me // PAIR, me % PAIR
    sib = x * 2 + (1 - core)
    across = (1 - x) * 2 + core
    diag = (1 - x) * 2 + (1 - core)
    y_peer = z * PAIR + (1 - y)

    barrier = pltpu.get_barrier_semaphore()
    for group in (sib, across, diag):
        pl.semaphore_signal(barrier, inc=1, device_id=(group, me), device_id_type=pl.DeviceIdType.MESH)
    for d in range(1, env):
        pl.semaphore_signal(barrier, inc=1, device_id=(league_me, (me + d) % env), device_id_type=pl.DeviceIdType.MESH)
    pl.semaphore_wait(barrier, 3 + env - 1)

    def remote(src, dst, send, recv, group, place):
        return pltpu.make_async_remote_copy(
            src_ref=src, dst_ref=dst, send_sem=send, recv_sem=recv,
            device_id=(group, place), device_id_type=pl.DeviceIdType.MESH,
        )

    def w_copy(b, line, way, place):
        slot = line * PAIR + y
        return remote(
            wbuf.at[b, slot], wbuf.at[b, slot], w_send.at[b, line, way], w_recv.at[b, slot], league_me, place
        )

    def to_right(b, line):
        return w_copy(b, line, 0, me + PAIR)

    def to_left(b, line):
        return w_copy(b, line, 1, me - PAIR)

    def to_y(b, line):
        return w_copy(b, line, 2, y_peer)

    def w_wait(b, slot):
        remote(
            wbuf.at[b, slot], wbuf.at[b, slot], w_send.at[b, 0, 2], w_recv.at[b, slot], league_me, y_peer
        ).wait_recv()

    def own_sends(b):
        @pl.when(z < LINE - 1)
        def _():
            to_right(b, z).start()

        @pl.when(z > 0)
        def _():
            to_left(b, z).start()

        to_y(b, z).start()

    def hops(b):
        for h in range(1, LINE):
            low, high = z - h, z + h

            @pl.when(low >= 0)
            def _():
                w_wait(b, low * PAIR + y)

                @pl.when(z < LINE - 1)
                def _():
                    to_right(b, low).start()

                to_y(b, low).start()

            @pl.when(high < LINE)
            def _():
                w_wait(b, high * PAIR + y)

                @pl.when(z > 0)
                def _():
                    to_left(b, high).start()

                to_y(b, high).start()

    def finish_w_sends(b):
        for line in range(LINE):
            @pl.when(jnp.logical_and(line <= z, z < LINE - 1))
            def _():
                to_right(b, line).wait_send()

            @pl.when(jnp.logical_and(line >= z, z > 0))
            def _():
                to_left(b, line).wait_send()

            to_y(b, line).wait_send()

    def o_copy(r, way):
        if way == 0:
            src, dst, group = opp_ref.at[r], rows.at[league_me, r], across
        elif way == 1:
            src, dst, group = opp_ref.at[r], rows.at[league_me, r], sib
        else:
            src, dst, group = rows.at[across, r], rows.at[across, r], sib
        return remote(src, dst, o_send.at[way, r], o_recv.at[way, r], group, me)

    def norm(src, dst, gain, tile=64):
        def step(i, _):
            at = pl.ds(pl.multiple_of(i * tile, tile), tile)
            v = src[at, :].astype(F32)
            scale = lax.rsqrt(jnp.mean(v * v, axis=-1, keepdims=True) + 1e-05)
            dst[at, :] = (v * scale * gain[...]).astype(BF16)
            return 0

        lax.fori_loop(0, count // tile, step, 0)

    for b in range(blocks):
        wbuf[b, me] = w_ref[:, b * width:(b + 1) * width]
    own_sends(0)
    picks_all[league_me] = picks_ref[...]
    pick_copies = [
        remote(picks_ref, picks_all.at[league_me], p_send.at[i], p_recv.at[i], group, me)
        for i, group in enumerate((sib, across, diag))
    ]
    for copy in pick_copies:
        copy.start()
    for r in range(rounds):
        o_copy(r, 0).start()
    for r in range(rounds):
        o_copy(r, 1).start()
    own_sends(1)
    for r in range(rounds):
        norm(own_ref.at[r], own_n.at[r], gain_ref)
    hops(0)
    own_sends(2)
    for r in range(rounds):
        norm(opp_ref.at[r], rows.at[league_me, r], gain_ref)
    for r in range(rounds):
        o_copy(r, 1).wait_recv()
        norm(rows.at[sib, r], rows.at[sib, r], gain_ref)
    hops(1)
    own_sends(3)

    def base(i, _):
        b, r = i // rounds, i % rounds
        cols = pl.ds(pl.multiple_of(b * width, width), width)
        acts = jnp.dot(onehot_ref[r], table_ref[:, cols], preferred_element_type=F32)
        joint[b, r] = own_ref[r, :, cols].astype(F32) + opp_ref[r, :, cols].astype(F32) + acts
        return 0

    lax.fori_loop(0, blocks * rounds, base, 0)
    for copy in pick_copies:
        copy.wait_recv()
    for r in range(rounds):
        o_copy(r, 0).wait_recv()
        o_copy(r, 2).start()
    for r in range(rounds):
        o_copy(r, 2).wait_recv()
        norm(rows.at[diag, r], rows.at[diag, r], gain_ref)
    for r in range(rounds):
        o_copy(r, 2).wait_send()
        norm(rows.at[across, r], rows.at[across, r], gain_ref)

    def s_copy(b, k):
        return remote(to_sib.at[b, k], from_sib.at[b, k], s_send.at[b, k], s_recv.at[b, k], sib, me)

    def x_copy(b):
        return remote(to_x.at[b], from_x.at[b], x_send.at[b], x_recv.at[b], across, me)

    mine = league_me.astype(F32)

    def each_round(body):
        def step(r, _):
            body(r)
            return 0

        lax.fori_loop(0, rounds, step, 0)

    def block(b, _):
        @pl.when(b + 2 < blocks)
        def _():
            hops(b + 2)

        for line in range(LINE):
            w_wait(b, line * PAIR + (1 - y))

        def dot(lhs):
            return jnp.dot(lhs, wbuf[b].reshape(env * depth, width), preferred_element_type=F32)

        def served(group, r):
            chosen = picks_all[group, pl.ds(r, 1), :][:, :1]
            return dot(rows[group, r]) * jnp.where(chosen == mine, 1.0, 0.0)

        def first(r):
            to_sib[b, 0, r] = served(diag, r).astype(BF16)

        each_round(first)
        s_copy(b, 0).start()

        def second(r):
            to_sib[b, 1, r] = served(sib, r).astype(BF16)

        each_round(second)
        s_copy(b, 1).start()

        def third(r):
            to_x[b, r] = served(across, r).astype(BF16)

        each_round(third)
        s_copy(b, 0).wait_recv()

        def combine(r):
            to_x[b, r] = to_x[b, r] + from_sib[b, 0, r]

        each_round(combine)
        x_copy(b).start()

        def fourth(r):
            joint[b, r] += dot(own_n[r])

        each_round(fourth)

        def fifth(r):
            joint[b, r] += served(league_me, r)

        each_round(fifth)
        s_copy(b, 1).wait_recv()

        def sixth(r):
            joint[b, r] += from_sib[b, 1, r].astype(F32)

        each_round(sixth)
        return 0

    lax.fori_loop(0, blocks, block, 0)

    row = lax.broadcasted_iota(jnp.int32, (count, count), 0)
    col = lax.broadcasted_iota(jnp.int32, (count, count), 1)
    order = jnp.where(col == (row % envs) * steps + row // envs, 1.0, 0.0).astype(BF16)
    share = model // env

    def a_copy(r, d):
        target = (me + d) % env
        return remote(
            jsend.at[target, r], arecv.at[r, :, me], a_send.at[r, d], a_recv.at[r, d], league_me, target
        )

    for b in range(blocks):
        x_copy(b).wait_recv()
    tile = 64

    def joint_round(r):
        def joint_tile(i, _):
            at = pl.ds(pl.multiple_of(i * tile, tile), tile)
            parts = [joint[b, r, at, :] + from_x[b, r, at, :].astype(F32) for b in range(blocks)]
            total = sum(jnp.sum(p * p, axis=-1, keepdims=True) for p in parts)
            scale = lax.rsqrt(total * (1.0 / model) + 1e-05)
            for b in range(blocks):
                cols = slice(b * width, (b + 1) * width)
                jrow[r, at, cols] = (parts[b] * scale * vgain_ref[:, cols]).astype(BF16)
            return 0

        lax.fori_loop(0, count // tile, joint_tile, 0)
        for e in range(env):
            moved = jnp.dot(order, jrow[r, :, e * share:(e + 1) * share], preferred_element_type=F32)
            jsend[e, r] = moved.astype(BF16).reshape(steps, envs, share)
        for d in range(1, env):
            a_copy(r, d).start()

    for r in range(rounds):
        joint_round(r)
    for r in range(rounds):
        arecv[r, :, me] = jsend[me, r]
        hidden = jnp.dot(jrow[r], up_ref[...], preferred_element_type=F32)
        hidden = (hidden / (1.0 + jnp.exp(-hidden))).astype(BF16)
        val_ref[r] = lax.dot_general(
            vout_ref[...], hidden, (((1,), (1,)), ((), ())), preferred_element_type=F32
        )
    frow = lax.broadcasted_iota(jnp.int32, (share, share), 0)
    fcol = lax.broadcasted_iota(jnp.int32, (share, share), 1)
    same = jnp.where(frow == fcol, 1.0, 0.0).astype(BF16)
    for r in range(rounds):
        for d in range(1, env):
            a_copy(r, d).wait_recv()

        def turn(t, _):
            piece = arecv[r, t].reshape(env * envs, share)
            out_ref[r, t] = lax.dot_general(
                same, piece, (((1,), (1,)), ((), ())), preferred_element_type=F32
            ).astype(BF16)
            return 0

        lax.fori_loop(0, steps, turn, 0)

    for b in range(blocks):
        finish_w_sends(b)
        s_copy(b, 0).wait_send()
        s_copy(b, 1).wait_send()
        x_copy(b).wait_send()
    for copy in pick_copies:
        copy.wait_send()
    for r in range(rounds):
        o_copy(r, 0).wait_send()
        o_copy(r, 1).wait_send()
        for d in range(1, env):
            a_copy(r, d).wait_send()


def fused(
    obs_own,
    obs_opp,
    actions,
    opponent_picks,
    policy_weight,
    policy_gain,
    action_table,
    value_gain,
    value_up,
    value_out,
):
    rounds, envs, steps, model = obs_own.shape[1:]
    count = envs * steps
    env = lax.axis_size("env")
    groups = lax.axis_size("league")
    depth = policy_weight.shape[1]
    width = model // BLOCKS
    share = model // env
    hidden = value_up.shape[1]
    action_range = jnp.arange(action_table.shape[0], dtype=jnp.int32)
    ids = actions[0].reshape(2, rounds, count)
    onehot = (ids[0][:, :, None] == action_range).astype(BF16) + (
        ids[1][:, :, None] == action_range
    ).astype(BF16)
    picks = jnp.zeros((8, 128), F32).at[:rounds].set(opponent_picks[0].astype(F32)[:, None])
    vmem = pl.BlockSpec(memory_space=pltpu.VMEM)
    dma = pltpu.SemaphoreType.DMA
    out, val = pl.pallas_call(
        window_kernel,
        out_shape=(
            jax.ShapeDtypeStruct((rounds, steps, share, env * envs), BF16),
            jax.ShapeDtypeStruct((rounds, 8, count), F32),
        ),
        in_specs=[vmem] * 10,
        out_specs=(vmem, vmem),
        scratch_shapes=[
            pltpu.VMEM((BLOCKS, env, depth, width), BF16),
            pltpu.VMEM((groups, rounds, count, model), BF16),
            pltpu.VMEM((rounds, count, model), BF16),
            pltpu.VMEM((BLOCKS, rounds, count, width), F32),
            pltpu.VMEM((BLOCKS, 2, rounds, count, width), BF16),
            pltpu.VMEM((BLOCKS, 2, rounds, count, width), BF16),
            pltpu.VMEM((BLOCKS, rounds, count, width), BF16),
            pltpu.VMEM((BLOCKS, rounds, count, width), BF16),
            pltpu.VMEM((groups, 8, 128), F32),
            pltpu.VMEM((rounds, count, model), BF16),
            pltpu.VMEM((env, rounds, steps, envs, share), BF16),
            pltpu.VMEM((rounds, steps, env, envs, share), BF16),
            dma((BLOCKS, LINE, 3)),
            dma((BLOCKS, env)),
            dma((3, rounds)),
            dma((3, rounds)),
            dma((3,)),
            dma((3,)),
            dma((BLOCKS, 2)),
            dma((BLOCKS, 2)),
            dma((BLOCKS,)),
            dma((BLOCKS,)),
            dma((rounds, env)),
            dma((rounds, env)),
        ],
        compiler_params=pltpu.CompilerParams(
            collective_id=0, has_side_effects=True, vmem_limit_bytes=62 * MIB
        ),
    )(
        policy_weight[0],
        obs_own[0].reshape(rounds, count, model),
        obs_opp[0].reshape(rounds, count, model),
        onehot,
        picks,
        policy_gain.astype(F32),
        action_table,
        value_gain.astype(F32)[None],
        value_up,
        jnp.broadcast_to(value_out[None], (8, hidden)),
    )
    values = val[:, 0].reshape(1, rounds, envs, steps)
    return (out[None], values)


def solution(mesh):
    in_specs = (
        P("league", None, "env", None, None),
        P("league", None, "env", None, None),
        P("league", None, None, "env", None),
        P("league", None),
        P("league", "env", None),
        P("league", None),
        P(),
        P(),
        P(),
        P(),
    )
    out_specs = (P("league", None, None, "env", None), P("league", None, "env", None))
    body = fused if mesh.shape["env"] == LINE * PAIR else local
    return jax.shard_map(body, mesh=mesh, in_specs=in_specs, out_specs=out_specs, check_vma=False)
```

```python
import functools

import jax
import jax.numpy as jnp
from jax import lax
from jax.experimental import pallas as pl
from jax.experimental.pallas import tpu as pltpu
from jax.sharding import PartitionSpec as P

F32 = jnp.float32
BF16 = jnp.bfloat16
BLOCKS = 4
LINE = 4
PAIR = 2
MIB = 1 << 20


def rms_norm(inputs, gain):
    scale = lax.rsqrt(jnp.mean(inputs * inputs, axis=-1, keepdims=True) + 1e-05)
    return inputs * scale * gain.astype(jnp.float32)


def local(
    obs_own,
    obs_opp,
    actions,
    opponent_picks,
    policy_weight,
    policy_gain,
    action_table,
    value_gain,
    value_up,
    value_out,
):
    round_count = obs_own.shape[1]
    env_count = obs_own.shape[2]
    step_count = obs_own.shape[3]
    model_width = obs_own.shape[4]
    row_count = env_count * step_count
    weight_shard = policy_weight[0]
    own_gain = policy_gain[0]
    group_count = lax.axis_size("league")
    my_group = lax.axis_index("league")
    own_inputs = obs_own[0].reshape(round_count * row_count, model_width).astype(jnp.float32)
    own_normed = rms_norm(own_inputs, own_gain).astype(jnp.bfloat16)
    own_whole = lax.all_gather(weight_shard, "env", axis=0, tiled=True)
    own_state = own_inputs + jnp.dot(own_normed, own_whole, preferred_element_type=jnp.float32)
    every_pick = lax.all_gather(opponent_picks, "league", axis=0, tiled=True)
    action_range = jnp.arange(action_table.shape[0], dtype=jnp.int32)
    traj_list = []
    value_list = []
    for round_index in range(round_count):
        opp_raw = obs_opp[0, round_index].reshape(row_count, model_width)
        opp_inputs = opp_raw.astype(jnp.float32)
        all_rows = lax.all_gather(opp_raw, "league", axis=0, tiled=True)
        all_normed = rms_norm(all_rows.astype(jnp.float32), own_gain).astype(jnp.bfloat16)
        products = jnp.dot(all_normed, own_whole, preferred_element_type=jnp.float32)
        served = (every_pick[:, round_index] == my_group).astype(jnp.float32)
        products = (
            products.reshape(group_count, row_count, model_width) * served[:, None, None]
        ).astype(jnp.bfloat16)
        answers = lax.all_to_all(products, "league", split_axis=0, concat_axis=0, tiled=True)
        opp_state = opp_inputs + jnp.sum(answers.astype(jnp.float32), axis=0)
        own_ids = actions[0, 0, round_index].reshape(row_count)
        opp_ids = actions[0, 1, round_index].reshape(row_count)
        onehot = (own_ids[:, None] == action_range[None, :]).astype(jnp.bfloat16) + (
            opp_ids[:, None] == action_range[None, :]
        ).astype(jnp.bfloat16)
        action_sum = jnp.dot(onehot, action_table, preferred_element_type=jnp.float32)
        round_state = lax.dynamic_slice_in_dim(own_state, round_index * row_count, row_count, 0)
        joint_sum = round_state + opp_state + action_sum
        joint_row = rms_norm(joint_sum, value_gain).astype(jnp.bfloat16)
        value_hidden = jax.nn.silu(
            jnp.dot(joint_row, value_up, preferred_element_type=jnp.float32)
        ).astype(jnp.bfloat16)
        value_est = jnp.dot(value_hidden, value_out, preferred_element_type=jnp.float32)
        value_list.append(value_est.reshape(env_count, step_count))
        time_block = joint_row.reshape(env_count, step_count, model_width).transpose(1, 2, 0)
        traj_list.append(lax.all_to_all(time_block, "env", split_axis=1, concat_axis=2, tiled=True))
    learner_rows = jnp.stack(traj_list)
    values = jnp.stack(value_list)
    return (learner_rows[None], values[None])


def window_kernel(
    w_ref, own_ref, opp_ref, onehot_ref, small_ref, table_ref, up_ref,
    out_ref, val_ref,
    wbuf, rows, own_n, joint, to_sib, from_sib, to_x, from_x, picks_all, jrow, jsend, arecv,
    w_send, w_recv, o_send, o_recv, p_send, p_recv, s_send, s_recv, x_send, x_recv, a_send, a_recv,
):
    blocks, env, depth, width = wbuf.shape
    rounds, count, model = own_ref.shape
    steps, envs = arecv.shape[1], arecv.shape[3]
    league_me = lax.axis_index("league")
    me = lax.axis_index("env")
    x, core = league_me // 2, league_me % 2
    z, y = me // PAIR, me % PAIR
    sib = x * 2 + (1 - core)
    across = (1 - x) * 2 + core
    diag = (1 - x) * 2 + (1 - core)
    y_peer = z * PAIR + (1 - y)

    barrier = pltpu.get_barrier_semaphore()
    for group in (sib, across, diag):
        pl.semaphore_signal(barrier, inc=1, device_id=(group, me), device_id_type=pl.DeviceIdType.MESH)
    for d in range(1, env):
        pl.semaphore_signal(barrier, inc=1, device_id=(league_me, (me + d) % env), device_id_type=pl.DeviceIdType.MESH)
    pl.semaphore_wait(barrier, 3 + env - 1)

    def remote(src, dst, send, recv, group, place):
        return pltpu.make_async_remote_copy(
            src_ref=src, dst_ref=dst, send_sem=send, recv_sem=recv,
            device_id=(group, place), device_id_type=pl.DeviceIdType.MESH,
        )

    def w_copy(b, line, way, place):
        slot = line * PAIR + y
        return remote(
            wbuf.at[b, slot], wbuf.at[b, slot], w_send.at[b, line, way], w_recv.at[b, slot], league_me, place
        )

    def to_right(b, line):
        return w_copy(b, line, 0, me + PAIR)

    def to_left(b, line):
        return w_copy(b, line, 1, me - PAIR)

    def to_y(b, line):
        return w_copy(b, line, 2, y_peer)

    def w_wait(b, slot):
        remote(
            wbuf.at[b, slot], wbuf.at[b, slot], w_send.at[b, 0, 2], w_recv.at[b, slot], league_me, y_peer
        ).wait_recv()

    def own_sends(b):
        @pl.when(z < LINE - 1)
        def _():
            to_right(b, z).start()

        @pl.when(z > 0)
        def _():
            to_left(b, z).start()

        to_y(b, z).start()

    def hop(b, h):
        low, high = z - h, z + h

        @pl.when(low >= 0)
        def _():
            w_wait(b, low * PAIR + y)

            @pl.when(z < LINE - 1)
            def _():
                to_right(b, low).start()

            to_y(b, low).start()

        @pl.when(high < LINE)
        def _():
            w_wait(b, high * PAIR + y)

            @pl.when(z > 0)
            def _():
                to_left(b, high).start()

            to_y(b, high).start()

    def hops(b):
        for h in range(1, LINE):
            hop(b, h)

    def finish_w_sends(b):
        for line in range(LINE):
            @pl.when(jnp.logical_and(line <= z, z < LINE - 1))
            def _():
                to_right(b, line).wait_send()

            @pl.when(jnp.logical_and(line >= z, z > 0))
            def _():
                to_left(b, line).wait_send()

            to_y(b, line).wait_send()

    def o_copy(r, way):
        if way == 0:
            src, dst, group = opp_ref.at[r], rows.at[league_me, r], across
        elif way == 1:
            src, dst, group = opp_ref.at[r], rows.at[league_me, r], sib
        else:
            src, dst, group = rows.at[across, r], rows.at[across, r], sib
        return remote(src, dst, o_send.at[way, r], o_recv.at[way, r], group, me)

    def norm(src, dst, gain, tile=64):
        def step(i, _):
            at = pl.ds(pl.multiple_of(i * tile, tile), tile)
            v = src[at, :].astype(F32)
            scale = lax.rsqrt(jnp.mean(v * v, axis=-1, keepdims=True) + 1e-05)
            dst[at, :] = (v * scale * gain).astype(BF16)
            return 0

        lax.fori_loop(0, count // tile, step, 0)

    gain = small_ref[0:1, :]
    tag = small_ref.at[:, 0:128]
    for b in range(blocks):
        wbuf[b, me] = w_ref[:, b * width:(b + 1) * width]
    own_sends(0)
    picks_all[league_me] = tag[...]
    pick_copies = [
        remote(tag, picks_all.at[league_me], p_send.at[i], p_recv.at[i], group, me)
        for i, group in enumerate((sib, across, diag))
    ]
    for copy in pick_copies:
        copy.start()
    for r in range(rounds):
        o_copy(r, 0).start()
    for r in range(rounds):
        o_copy(r, 1).start()
    own_sends(1)
    for r in range(rounds):
        norm(own_ref.at[r], own_n.at[r], gain)
    hops(0)
    own_sends(2)
    for r in range(rounds):
        norm(opp_ref.at[r], rows.at[league_me, r], gain)
    hops(1)
    own_sends(3)
    for r in range(rounds):
        o_copy(r, 1).wait_recv()
        norm(rows.at[sib, r], rows.at[sib, r], gain)

    def base(i, _):
        b, r = i // rounds, i % rounds
        cols = pl.ds(pl.multiple_of(b * width, width), width)
        acts = jnp.dot(onehot_ref[r], table_ref[:, cols], preferred_element_type=F32)
        joint[b, r] = own_ref[r, :, cols].astype(F32) + opp_ref[r, :, cols].astype(F32) + acts
        return 0

    lax.fori_loop(0, blocks * rounds, base, 0)
    for copy in pick_copies:
        copy.wait_recv()

    def s_copy(b, r, k):
        return remote(to_sib.at[b, k, r], from_sib.at[b, k, r], s_send.at[b, r, k], s_recv.at[b, r, k], sib, me)

    def x_copy(b, r):
        return remote(to_x.at[b, r], from_x.at[b, r], x_send.at[b, r], x_recv.at[b, r], across, me)

    mine = league_me.astype(F32)

    def unit(i, _):
        b, r = i // rounds, i % rounds

        @pl.when(i < (blocks - 2) * (LINE - 1))
        def _():
            hop(2 + i // (LINE - 1), i % (LINE - 1) + 1)

        @pl.when(i < rounds)
        def _():
            o_copy(r, 0).wait_recv()
            o_copy(r, 2).start()
            o_copy(r, 2).wait_recv()
            norm(rows.at[diag, r], rows.at[diag, r], gain)
            o_copy(r, 2).wait_send()
            norm(rows.at[across, r], rows.at[across, r], gain)

        @pl.when(r == 0)
        def _():
            for line in range(LINE):
                w_wait(b, line * PAIR + (1 - y))

        def dot(lhs):
            return jnp.dot(lhs, wbuf[b].reshape(env * depth, width), preferred_element_type=F32)

        def served(group):
            chosen = jnp.where(r == 0, picks_all[group, 3:4, :], picks_all[group, 4:5, :])[:, :1]
            return dot(rows[group, r]) * jnp.where(chosen == mine, 1.0, 0.0)

        to_sib[b, 0, r] = served(diag).astype(BF16)
        s_copy(b, r, 0).start()
        to_sib[b, 1, r] = served(sib).astype(BF16)
        s_copy(b, r, 1).start()
        to_x[b, r] = served(across).astype(BF16)
        s_copy(b, r, 0).wait_recv()
        to_x[b, r] = to_x[b, r] + from_sib[b, 0, r]
        x_copy(b, r).start()
        joint[b, r] += dot(own_n[r])
        joint[b, r] += served(league_me)
        return 0

    lax.fori_loop(0, blocks * rounds, unit, 0)

    row = lax.broadcasted_iota(jnp.int32, (count, count), 0)
    col = lax.broadcasted_iota(jnp.int32, (count, count), 1)
    order = jnp.where(col == (row % envs) * steps + row // envs, 1.0, 0.0).astype(BF16)
    share = model // env

    def a_copy(r, d):
        target = (me + d) % env
        return remote(
            jsend.at[target, r], arecv.at[r, :, me], a_send.at[r, d], a_recv.at[r, d], league_me, target
        )

    tile = 64

    def joint_round(r):
        for b in range(blocks):
            s_copy(b, r, 1).wait_recv()
            x_copy(b, r).wait_recv()

        def joint_tile(i, _):
            at = pl.ds(pl.multiple_of(i * tile, tile), tile)
            parts = [
                joint[b, r, at, :] + from_sib[b, 1, r, at, :].astype(F32) + from_x[b, r, at, :].astype(F32)
                for b in range(blocks)
            ]
            total = sum(jnp.sum(p * p, axis=-1, keepdims=True) for p in parts)
            scale = lax.rsqrt(total * (1.0 / model) + 1e-05)
            for b in range(blocks):
                cols = slice(b * width, (b + 1) * width)
                jrow[r, at, cols] = (parts[b] * scale * small_ref[1:2, cols]).astype(BF16)
            return 0

        lax.fori_loop(0, count // tile, joint_tile, 0)
        for e in range(env):
            moved = jnp.dot(order, jrow[r, :, e * share:(e + 1) * share], preferred_element_type=F32)
            jsend[e, r] = moved.astype(BF16).reshape(steps, envs, share)
        for d in range(1, env):
            a_copy(r, d).start()

    for r in range(rounds):
        joint_round(r)
    for r in range(rounds):
        arecv[r, :, me] = jsend[me, r]
        hidden = jnp.dot(jrow[r], up_ref[...], preferred_element_type=F32)
        hidden = (hidden / (1.0 + jnp.exp(-hidden))).astype(BF16)
        out_row = jnp.broadcast_to(small_ref[2:3, :up_ref.shape[1]], (8, up_ref.shape[1])).astype(BF16)
        val_ref[r] = lax.dot_general(
            out_row, hidden, (((1,), (1,)), ((), ())), preferred_element_type=F32
        )[0:1]
    frow = lax.broadcasted_iota(jnp.int32, (share, share), 0)
    fcol = lax.broadcasted_iota(jnp.int32, (share, share), 1)
    same = jnp.where(frow == fcol, 1.0, 0.0).astype(BF16)
    for r in range(rounds):
        for d in range(1, env):
            a_copy(r, d).wait_recv()

        def turn(t, _):
            piece = arecv[r, t].reshape(env * envs, share)
            out_ref[r, t] = lax.dot_general(
                same, piece, (((1,), (1,)), ((), ())), preferred_element_type=F32
            ).astype(BF16)
            return 0

        lax.fori_loop(0, steps, turn, 0)

    for b in range(blocks):
        finish_w_sends(b)
        for r in range(rounds):
            s_copy(b, r, 0).wait_send()
            s_copy(b, r, 1).wait_send()
            x_copy(b, r).wait_send()
    for copy in pick_copies:
        copy.wait_send()
    for r in range(rounds):
        o_copy(r, 0).wait_send()
        o_copy(r, 1).wait_send()
        for d in range(1, env):
            a_copy(r, d).wait_send()


def fused(
    obs_own,
    obs_opp,
    actions,
    opponent_picks,
    policy_weight,
    policy_gain,
    action_table,
    value_gain,
    value_up,
    value_out,
):
    rounds, envs, steps, model = obs_own.shape[1:]
    count = envs * steps
    env = lax.axis_size("env")
    groups = lax.axis_size("league")
    depth = policy_weight.shape[1]
    width = model // BLOCKS
    share = model // env
    hidden = value_up.shape[1]
    action_range = jnp.arange(action_table.shape[0], dtype=jnp.int32)
    ids = actions[0].reshape(2, rounds, count)
    onehot = (ids[0][:, :, None] == action_range).astype(BF16) + (
        ids[1][:, :, None] == action_range
    ).astype(BF16)
    small = jnp.concatenate(
        [
            policy_gain.astype(F32),
            value_gain.astype(F32)[None],
            jnp.pad(value_out.astype(F32), (0, model - hidden))[None],
            jnp.broadcast_to(opponent_picks[0].astype(F32)[:, None], (rounds, model)),
            jnp.zeros((5 - rounds, model), F32),
        ]
    )
    vmem = pl.BlockSpec(memory_space=pltpu.VMEM)
    dma = pltpu.SemaphoreType.DMA
    out, val = pl.pallas_call(
        window_kernel,
        out_shape=(
            jax.ShapeDtypeStruct((rounds, steps, share, env * envs), BF16),
            jax.ShapeDtypeStruct((rounds, 1, count), F32),
        ),
        in_specs=[vmem] * 7,
        out_specs=(vmem, vmem),
        scratch_shapes=[
            pltpu.VMEM((BLOCKS, env, depth, width), BF16),
            pltpu.VMEM((groups, rounds, count, model), BF16),
            pltpu.VMEM((rounds, count, model), BF16),
            pltpu.VMEM((BLOCKS, rounds, count, width), F32),
            pltpu.VMEM((BLOCKS, 2, rounds, count, width), BF16),
            pltpu.VMEM((BLOCKS, 2, rounds, count, width), BF16),
            pltpu.VMEM((BLOCKS, rounds, count, width), BF16),
            pltpu.VMEM((BLOCKS, rounds, count, width), BF16),
            pltpu.VMEM((groups, 8, 128), F32),
            pltpu.VMEM((rounds, count, model), BF16),
            pltpu.VMEM((env, rounds, steps, envs, share), BF16),
            pltpu.VMEM((rounds, steps, env, envs, share), BF16),
            dma((BLOCKS, LINE, 3)),
            dma((BLOCKS, env)),
            dma((3, rounds)),
            dma((3, rounds)),
            dma((3,)),
            dma((3,)),
            dma((BLOCKS, rounds, 2)),
            dma((BLOCKS, rounds, 2)),
            dma((BLOCKS, rounds)),
            dma((BLOCKS, rounds)),
            dma((rounds, env)),
            dma((rounds, env)),
        ],
        compiler_params=pltpu.CompilerParams(
            collective_id=0, has_side_effects=True, vmem_limit_bytes=62 * MIB
        ),
    )(
        policy_weight[0],
        obs_own[0].reshape(rounds, count, model),
        obs_opp[0].reshape(rounds, count, model),
        onehot,
        small,
        action_table,
        value_up,
    )
    values = val.reshape(1, rounds, envs, steps)
    return (out[None], values)


def solution(mesh):
    in_specs = (
        P("league", None, "env", None, None),
        P("league", None, "env", None, None),
        P("league", None, None, "env", None),
        P("league", None),
        P("league", "env", None),
        P("league", None),
        P(),
        P(),
        P(),
        P(),
    )
    out_specs = (P("league", None, None, "env", None), P("league", None, "env", None))
    body = fused if mesh.shape["env"] == LINE * PAIR else local
    return jax.shard_map(body, mesh=mesh, in_specs=in_specs, out_specs=out_specs, check_vma=False)
```

```python
import functools

import jax
import jax.numpy as jnp
from jax import lax
from jax.experimental import pallas as pl
from jax.experimental.pallas import tpu as pltpu
from jax.sharding import PartitionSpec as P

F32 = jnp.float32
BF16 = jnp.bfloat16
BLOCKS = 4
LINE = 4
PAIR = 2
MIB = 1 << 20


def rms_norm(inputs, gain):
    scale = lax.rsqrt(jnp.mean(inputs * inputs, axis=-1, keepdims=True) + 1e-05)
    return inputs * scale * gain.astype(jnp.float32)


def local(
    obs_own,
    obs_opp,
    actions,
    opponent_picks,
    policy_weight,
    policy_gain,
    action_table,
    value_gain,
    value_up,
    value_out,
):
    round_count = obs_own.shape[1]
    env_count = obs_own.shape[2]
    step_count = obs_own.shape[3]
    model_width = obs_own.shape[4]
    row_count = env_count * step_count
    weight_shard = policy_weight[0]
    own_gain = policy_gain[0]
    group_count = lax.axis_size("league")
    my_group = lax.axis_index("league")
    own_inputs = obs_own[0].reshape(round_count * row_count, model_width).astype(jnp.float32)
    own_normed = rms_norm(own_inputs, own_gain).astype(jnp.bfloat16)
    own_whole = lax.all_gather(weight_shard, "env", axis=0, tiled=True)
    own_state = own_inputs + jnp.dot(own_normed, own_whole, preferred_element_type=jnp.float32)
    every_pick = lax.all_gather(opponent_picks, "league", axis=0, tiled=True)
    action_range = jnp.arange(action_table.shape[0], dtype=jnp.int32)
    traj_list = []
    value_list = []
    for round_index in range(round_count):
        opp_raw = obs_opp[0, round_index].reshape(row_count, model_width)
        opp_inputs = opp_raw.astype(jnp.float32)
        all_rows = lax.all_gather(opp_raw, "league", axis=0, tiled=True)
        all_normed = rms_norm(all_rows.astype(jnp.float32), own_gain).astype(jnp.bfloat16)
        products = jnp.dot(all_normed, own_whole, preferred_element_type=jnp.float32)
        served = (every_pick[:, round_index] == my_group).astype(jnp.float32)
        products = (
            products.reshape(group_count, row_count, model_width) * served[:, None, None]
        ).astype(jnp.bfloat16)
        answers = lax.all_to_all(products, "league", split_axis=0, concat_axis=0, tiled=True)
        opp_state = opp_inputs + jnp.sum(answers.astype(jnp.float32), axis=0)
        own_ids = actions[0, 0, round_index].reshape(row_count)
        opp_ids = actions[0, 1, round_index].reshape(row_count)
        onehot = (own_ids[:, None] == action_range[None, :]).astype(jnp.bfloat16) + (
            opp_ids[:, None] == action_range[None, :]
        ).astype(jnp.bfloat16)
        action_sum = jnp.dot(onehot, action_table, preferred_element_type=jnp.float32)
        round_state = lax.dynamic_slice_in_dim(own_state, round_index * row_count, row_count, 0)
        joint_sum = round_state + opp_state + action_sum
        joint_row = rms_norm(joint_sum, value_gain).astype(jnp.bfloat16)
        value_hidden = jax.nn.silu(
            jnp.dot(joint_row, value_up, preferred_element_type=jnp.float32)
        ).astype(jnp.bfloat16)
        value_est = jnp.dot(value_hidden, value_out, preferred_element_type=jnp.float32)
        value_list.append(value_est.reshape(env_count, step_count))
        time_block = joint_row.reshape(env_count, step_count, model_width).transpose(1, 2, 0)
        traj_list.append(lax.all_to_all(time_block, "env", split_axis=1, concat_axis=2, tiled=True))
    learner_rows = jnp.stack(traj_list)
    values = jnp.stack(value_list)
    return (learner_rows[None], values[None])


def window_kernel(
    w_ref, own_ref, opp_ref, onehot_ref, small_ref, table_ref, up_ref,
    out_ref, val_ref,
    wbuf, rows, own_n, joint, to_sib, from_sib, to_x, from_x, picks_all, jrow, jsend, arecv,
    w_send, w_recv, o_send, o_recv, p_send, p_recv, s_send, s_recv, x_send, x_recv, a_send, a_recv,
):
    blocks, env, depth, width = wbuf.shape
    rounds, count, model = own_ref.shape
    steps, envs = arecv.shape[1], arecv.shape[3]
    league_me = lax.axis_index("league")
    me = lax.axis_index("env")
    x, core = league_me // 2, league_me % 2
    z, y = me // PAIR, me % PAIR
    sib = x * 2 + (1 - core)
    across = (1 - x) * 2 + core
    diag = (1 - x) * 2 + (1 - core)
    y_peer = z * PAIR + (1 - y)

    barrier = pltpu.get_barrier_semaphore()
    for group in (sib, across, diag):
        pl.semaphore_signal(barrier, inc=1, device_id=(group, me), device_id_type=pl.DeviceIdType.MESH)
    for d in range(1, env):
        pl.semaphore_signal(barrier, inc=1, device_id=(league_me, (me + d) % env), device_id_type=pl.DeviceIdType.MESH)
    pl.semaphore_wait(barrier, 3 + env - 1)

    def remote(src, dst, send, recv, group, place):
        return pltpu.make_async_remote_copy(
            src_ref=src, dst_ref=dst, send_sem=send, recv_sem=recv,
            device_id=(group, place), device_id_type=pl.DeviceIdType.MESH,
        )

    def w_copy(b, line, way, place):
        slot = line * PAIR + y
        return remote(
            wbuf.at[b, slot], wbuf.at[b, slot], w_send.at[b, line, way], w_recv.at[b, slot], league_me, place
        )

    def to_right(b, line):
        return w_copy(b, line, 0, me + PAIR)

    def to_left(b, line):
        return w_copy(b, line, 1, me - PAIR)

    def to_y(b, line):
        return w_copy(b, line, 2, y_peer)

    def w_wait(b, slot):
        remote(
            wbuf.at[b, slot], wbuf.at[b, slot], w_send.at[b, 0, 2], w_recv.at[b, slot], league_me, y_peer
        ).wait_recv()

    def own_sends(b):
        @pl.when(z < LINE - 1)
        def _():
            to_right(b, z).start()

        @pl.when(z > 0)
        def _():
            to_left(b, z).start()

        to_y(b, z).start()

    def hop(b, h):
        low, high = z - h, z + h

        @pl.when(low >= 0)
        def _():
            w_wait(b, low * PAIR + y)

            @pl.when(z < LINE - 1)
            def _():
                to_right(b, low).start()

            to_y(b, low).start()

        @pl.when(high < LINE)
        def _():
            w_wait(b, high * PAIR + y)

            @pl.when(z > 0)
            def _():
                to_left(b, high).start()

            to_y(b, high).start()

    def hops(b):
        for h in range(1, LINE):
            hop(b, h)

    def finish_w_sends(b):
        for line in range(LINE):
            @pl.when(jnp.logical_and(line <= z, z < LINE - 1))
            def _():
                to_right(b, line).wait_send()

            @pl.when(jnp.logical_and(line >= z, z > 0))
            def _():
                to_left(b, line).wait_send()

            to_y(b, line).wait_send()

    def o_copy(r, way):
        if way == 0:
            src, dst, group = opp_ref.at[r], rows.at[league_me, r], across
        elif way == 1:
            src, dst, group = opp_ref.at[r], rows.at[league_me, r], sib
        else:
            src, dst, group = rows.at[across, r], rows.at[across, r], sib
        return remote(src, dst, o_send.at[way, r], o_recv.at[way, r], group, me)

    def norm(src, dst, gain, tile=64):
        def step(i, _):
            at = pl.ds(pl.multiple_of(i * tile, tile), tile)
            v = src[at, :].astype(F32)
            scale = lax.rsqrt(jnp.mean(v * v, axis=-1, keepdims=True) + 1e-05)
            dst[at, :] = (v * scale * gain).astype(BF16)
            return 0

        lax.fori_loop(0, count // tile, step, 0)

    gain = small_ref[0:1, :]
    tag = small_ref.at[:, 0:128]
    for b in range(blocks):
        wbuf[b, me] = w_ref[:, b * width:(b + 1) * width]
    own_sends(0)
    picks_all[league_me] = tag[...]
    pick_copies = [
        remote(tag, picks_all.at[league_me], p_send.at[i], p_recv.at[i], group, me)
        for i, group in enumerate((sib, across, diag))
    ]
    for copy in pick_copies:
        copy.start()
    for r in range(rounds):
        o_copy(r, 0).start()
    for r in range(rounds):
        o_copy(r, 1).start()
    own_sends(1)
    for r in range(rounds):
        norm(own_ref.at[r], own_n.at[r], gain)
    hops(0)
    own_sends(2)
    for r in range(rounds):
        norm(opp_ref.at[r], rows.at[league_me, r], gain)
    hops(1)
    own_sends(3)
    for r in range(rounds):
        o_copy(r, 1).wait_recv()
        norm(rows.at[sib, r], rows.at[sib, r], gain)

    def base(i, _):
        b, r = i // rounds, i % rounds
        cols = pl.ds(pl.multiple_of(b * width, width), width)
        acts = jnp.dot(onehot_ref[r], table_ref[:, cols], preferred_element_type=F32)
        joint[b, r] = own_ref[r, :, cols].astype(F32) + opp_ref[r, :, cols].astype(F32) + acts
        return 0

    hops(2)
    lax.fori_loop(0, blocks * rounds, base, 0)
    for copy in pick_copies:
        copy.wait_recv()

    def s_copy(b, r, k):
        return remote(to_sib.at[b, k, r], from_sib.at[b, k, r], s_send.at[b, r, k], s_recv.at[b, r, k], sib, me)

    def x_copy(b, r):
        return remote(to_x.at[b, r], from_x.at[b, r], x_send.at[b, r], x_recv.at[b, r], across, me)

    mine = league_me.astype(F32)

    def unit(i, _):
        late = i // (2 * rounds)
        b = (1 - late) * (i % 2) + late * (i // rounds)
        r = (1 - late) * (i // 2) + late * (i % rounds)

        @pl.when(i < LINE - 1)
        def _():
            hop(3, i + 1)

        @pl.when(jnp.logical_and(i < 2 * rounds, b == 0))
        def _():
            o_copy(r, 0).wait_recv()
            o_copy(r, 2).start()
            o_copy(r, 2).wait_recv()
            norm(rows.at[diag, r], rows.at[diag, r], gain)
            o_copy(r, 2).wait_send()
            norm(rows.at[across, r], rows.at[across, r], gain)

        @pl.when(r == 0)
        def _():
            for line in range(LINE):
                w_wait(b, line * PAIR + (1 - y))

        def dot(lhs):
            return jnp.dot(lhs, wbuf[b].reshape(env * depth, width), preferred_element_type=F32)

        def served(group):
            chosen = jnp.where(r == 0, picks_all[group, 3:4, :], picks_all[group, 4:5, :])[:, :1]
            return dot(rows[group, r]) * jnp.where(chosen == mine, 1.0, 0.0)

        to_sib[b, 0, r] = served(diag).astype(BF16)
        s_copy(b, r, 0).start()
        to_sib[b, 1, r] = served(sib).astype(BF16)
        s_copy(b, r, 1).start()
        to_x[b, r] = served(across).astype(BF16)
        s_copy(b, r, 0).wait_recv()
        to_x[b, r] = to_x[b, r] + from_sib[b, 0, r]
        x_copy(b, r).start()
        joint[b, r] += dot(own_n[r])
        joint[b, r] += served(league_me)
        return 0

    lax.fori_loop(0, blocks * rounds, unit, 0)

    row = lax.broadcasted_iota(jnp.int32, (count, count), 0)
    col = lax.broadcasted_iota(jnp.int32, (count, count), 1)
    order = jnp.where(col == (row % envs) * steps + row // envs, 1.0, 0.0).astype(BF16)
    share = model // env

    def a_copy(r, d):
        target = (me + d) % env
        return remote(
            jsend.at[target, r], arecv.at[r, :, me], a_send.at[r, d], a_recv.at[r, d], league_me, target
        )

    tile = 64

    def joint_round(r):
        for b in range(blocks):
            s_copy(b, r, 1).wait_recv()
            x_copy(b, r).wait_recv()

        def joint_tile(i, _):
            at = pl.ds(pl.multiple_of(i * tile, tile), tile)
            parts = [
                joint[b, r, at, :] + from_sib[b, 1, r, at, :].astype(F32) + from_x[b, r, at, :].astype(F32)
                for b in range(blocks)
            ]
            total = sum(jnp.sum(p * p, axis=-1, keepdims=True) for p in parts)
            scale = lax.rsqrt(total * (1.0 / model) + 1e-05)
            for b in range(blocks):
                cols = slice(b * width, (b + 1) * width)
                jrow[r, at, cols] = (parts[b] * scale * small_ref[1:2, cols]).astype(BF16)
            return 0

        lax.fori_loop(0, count // tile, joint_tile, 0)
        for e in range(env):
            moved = jnp.dot(order, jrow[r, :, e * share:(e + 1) * share], preferred_element_type=F32)
            jsend[e, r] = moved.astype(BF16).reshape(steps, envs, share)
        for d in range(1, env):
            a_copy(r, d).start()

    for r in range(rounds):
        joint_round(r)
    for r in range(rounds):
        arecv[r, :, me] = jsend[me, r]
        hidden = jnp.dot(jrow[r], up_ref[...], preferred_element_type=F32)
        hidden = (hidden / (1.0 + jnp.exp(-hidden))).astype(BF16)
        out_row = jnp.broadcast_to(small_ref[2:3, :up_ref.shape[1]], (8, up_ref.shape[1])).astype(BF16)
        val_ref[r] = lax.dot_general(
            out_row, hidden, (((1,), (1,)), ((), ())), preferred_element_type=F32
        )[0:1]
    frow = lax.broadcasted_iota(jnp.int32, (share, share), 0)
    fcol = lax.broadcasted_iota(jnp.int32, (share, share), 1)
    same = jnp.where(frow == fcol, 1.0, 0.0).astype(BF16)
    for r in range(rounds):
        for d in range(1, env):
            a_copy(r, d).wait_recv()

        def turn(t, _):
            piece = arecv[r, t].reshape(env * envs, share)
            out_ref[r, t] = lax.dot_general(
                same, piece, (((1,), (1,)), ((), ())), preferred_element_type=F32
            ).astype(BF16)
            return 0

        lax.fori_loop(0, steps, turn, 0)

    for b in range(blocks):
        finish_w_sends(b)
        for r in range(rounds):
            s_copy(b, r, 0).wait_send()
            s_copy(b, r, 1).wait_send()
            x_copy(b, r).wait_send()
    for copy in pick_copies:
        copy.wait_send()
    for r in range(rounds):
        o_copy(r, 0).wait_send()
        o_copy(r, 1).wait_send()
        for d in range(1, env):
            a_copy(r, d).wait_send()


def fused(
    obs_own,
    obs_opp,
    actions,
    opponent_picks,
    policy_weight,
    policy_gain,
    action_table,
    value_gain,
    value_up,
    value_out,
):
    rounds, envs, steps, model = obs_own.shape[1:]
    count = envs * steps
    env = lax.axis_size("env")
    groups = lax.axis_size("league")
    depth = policy_weight.shape[1]
    width = model // BLOCKS
    share = model // env
    hidden = value_up.shape[1]
    action_range = jnp.arange(action_table.shape[0], dtype=jnp.int32)
    ids = actions[0].reshape(2, rounds, count)
    onehot = (ids[0][:, :, None] == action_range).astype(BF16) + (
        ids[1][:, :, None] == action_range
    ).astype(BF16)
    small = jnp.concatenate(
        [
            policy_gain.astype(F32),
            value_gain.astype(F32)[None],
            jnp.pad(value_out.astype(F32), (0, model - hidden))[None],
            jnp.broadcast_to(opponent_picks[0].astype(F32)[:, None], (rounds, model)),
            jnp.zeros((5 - rounds, model), F32),
        ]
    )
    vmem = pl.BlockSpec(memory_space=pltpu.VMEM)
    dma = pltpu.SemaphoreType.DMA
    out, val = pl.pallas_call(
        window_kernel,
        out_shape=(
            jax.ShapeDtypeStruct((rounds, steps, share, env * envs), BF16),
            jax.ShapeDtypeStruct((rounds, 1, count), F32),
        ),
        in_specs=[vmem] * 7,
        out_specs=(vmem, vmem),
        scratch_shapes=[
            pltpu.VMEM((BLOCKS, env, depth, width), BF16),
            pltpu.VMEM((groups, rounds, count, model), BF16),
            pltpu.VMEM((rounds, count, model), BF16),
            pltpu.VMEM((BLOCKS, rounds, count, width), F32),
            pltpu.VMEM((BLOCKS, 2, rounds, count, width), BF16),
            pltpu.VMEM((BLOCKS, 2, rounds, count, width), BF16),
            pltpu.VMEM((BLOCKS, rounds, count, width), BF16),
            pltpu.VMEM((BLOCKS, rounds, count, width), BF16),
            pltpu.VMEM((groups, 8, 128), F32),
            pltpu.VMEM((rounds, count, model), BF16),
            pltpu.VMEM((env, rounds, steps, envs, share), BF16),
            pltpu.VMEM((rounds, steps, env, envs, share), BF16),
            dma((BLOCKS, LINE, 3)),
            dma((BLOCKS, env)),
            dma((3, rounds)),
            dma((3, rounds)),
            dma((3,)),
            dma((3,)),
            dma((BLOCKS, rounds, 2)),
            dma((BLOCKS, rounds, 2)),
            dma((BLOCKS, rounds)),
            dma((BLOCKS, rounds)),
            dma((rounds, env)),
            dma((rounds, env)),
        ],
        compiler_params=pltpu.CompilerParams(
            collective_id=0, has_side_effects=True, vmem_limit_bytes=62 * MIB
        ),
    )(
        policy_weight[0],
        obs_own[0].reshape(rounds, count, model),
        obs_opp[0].reshape(rounds, count, model),
        onehot,
        small,
        action_table,
        value_up,
    )
    values = val.reshape(1, rounds, envs, steps)
    return (out[None], values)


def solution(mesh):
    in_specs = (
        P("league", None, "env", None, None),
        P("league", None, "env", None, None),
        P("league", None, None, "env", None),
        P("league", None),
        P("league", "env", None),
        P("league", None),
        P(),
        P(),
        P(),
        P(),
    )
    out_specs = (P("league", None, None, "env", None), P("league", None, "env", None))
    body = fused if mesh.shape["env"] == LINE * PAIR else local
    return jax.shard_map(body, mesh=mesh, in_specs=in_specs, out_specs=out_specs, check_vma=False)
```
